256 devices in a mesh: pb: 8 (over x, y_lo), ka: 4 (over y_hi, core), ha: 8 (over z).
Axes of the slice: x: 4, y: 4 (y_hi: 2, y_lo: 2; y = y_hi * 2 + y_lo), z: 8, core: 2. Of those that a mesh axis runs over, the one named last changes fastest.
Arguments:
- queries: bfloat16 [4096, 64, 128], P(('pb', 'ka'), 'ha'), may hold values from -8 to 8
- keys: bfloat16 [4096, 8, 128], P(('pb', 'ka'), 'ha'), may hold values from -4.5 to 4.5
- values: bfloat16 [4096, 8, 128], P(('pb', 'ka'), 'ha'), may hold values from -12 to 12
- out_grad: bfloat16 [4096, 64, 128], P(('pb', 'ka'), 'ha'), may hold values from -6 to 6
Outputs:
- attended: bfloat16 [4096, 64, 128], P(('pb', 'ka'), 'ha')
- query_grad: bfloat16 [4096, 64, 128], P(('pb', 'ka'), 'ha')
- key_grad: bfloat16 [4096, 8, 128], P(('pb', 'ka'), 'ha')
- value_grad: bfloat16 [4096, 8, 128], P(('pb', 'ka'), 'ha')
The draws below stay inside these ranges and needn't reach their ends.
All inputs are finite; a program needn't handle non-finite values.
Results may differ from the reference program's by a relative error of at most 0.0097.
Values may be sent and summed in bfloat16 or wider, within the bound.
No kernel may reach another device: no remote copies, remote signals or barrier semaphores. Data moves between devices by JAX's collectives and lax.ppermute only.
A program may use at most 128 MiB of HBM per device.

```python
import math
import jax
import jax.numpy as jnp
from jax import lax

HEADS = 64
KV_HEADS = 8
HEAD_DIM = 128
GROUP = 8
SEQUENCE = 4096


def draw_queries(key, part):
    noise_key = jax.random.fold_in(key, 11)
    full_shape = (SEQUENCE, HEADS, HEAD_DIM)
    sample = jnp.clip(2.0 * jax.random.normal(noise_key, full_shape, jnp.float32), -8.0, 8.0)
    return sample.astype(jnp.bfloat16)


def draw_keys(key, part):
    noise_key = jax.random.fold_in(key, 13)
    full_shape = (SEQUENCE, KV_HEADS, HEAD_DIM)
    sample = jnp.clip(jax.random.normal(noise_key, full_shape, jnp.float32), -4.5, 4.5)
    return sample.astype(jnp.bfloat16)


def shard_levels(own_key, extent, shards, least, largest):
    def one(axis_at, blocks):
        heights = jax.random.uniform(jax.random.fold_in(jax.random.fold_in(own_key, 6), axis_at), (blocks,), jnp.float32, least / len(shards), largest / len(shards))
        return jnp.repeat(jnp.exp(heights), extent[axis_at] // blocks).reshape((-1,) + (1,) * (len(extent) - axis_at - 1))

    level = one(*shards[0])
    for cut in shards[1:]:
        level = level * one(*cut)
    return level


def gaussian(key, shape, width, most, cuts=(), kind=jnp.bfloat16):
    level = shard_levels(key, shape, cuts, -0.22, 0.18) if cuts else 1.0
    values = jax.random.normal(key, shape, jnp.float32) * width * level
    return jnp.minimum(jnp.maximum(values, -most), most).astype(kind)


def setup_inputs(seed: int = 0) -> dict:
    key_list = jax.random.split(jax.random.key(seed), 5)
    queries = draw_queries(jax.random.fold_in(key_list[4], 71), 0)
    keys = draw_keys(jax.random.fold_in(key_list[4], 71), 0)
    values = gaussian(key_list[2], (SEQUENCE, KV_HEADS, HEAD_DIM), 2.0, 12.0, ((0, 32), (1, 8)))
    out_grad = gaussian(key_list[3], (SEQUENCE, HEADS, HEAD_DIM), 1.0, 6.0, ((0, 32), (1, 8)))
    return {"queries": queries, "keys": keys, "values": values, "out_grad": out_grad}


def round_half(tensor):
    return lax.optimization_barrier(tensor.astype(jnp.bfloat16)).astype(jnp.float32)


def one_head(inputs):
    query_head, key_head, value_head, grad_head = inputs
    scaling = HEAD_DIM ** -0.5
    total_rows = query_head.shape[0]
    block_rows = math.gcd(total_rows, 512)
    key_float = key_head.astype(jnp.float32)
    value_float = value_head.astype(jnp.float32)

    def visit_block(running, position):
        key_sum, value_sum = running
        first_row = position * block_rows
        query_block = lax.dynamic_slice_in_dim(query_head, first_row, block_rows, 0).astype(jnp.float32)
        grad_block = lax.dynamic_slice_in_dim(grad_head, first_row, block_rows, 0).astype(jnp.float32)
        scores = jnp.einsum('qgd,kd->gqk', query_block, key_float) * scaling
        row_max = jnp.max(scores, axis=-1)
        weights = jnp.exp(scores - row_max[..., None])
        row_total = jnp.sum(weights, axis=-1)
        exact_out = jnp.einsum('gqk,kd->gqd', weights, value_float,
                               precision=lax.Precision.HIGHEST) / row_total[..., None]
        output_block = exact_out.astype(jnp.bfloat16)
        log_total = row_max + jnp.log(row_total)
        row_dots = jnp.einsum('gqd,qgd->gq', exact_out, grad_block)
        probs = jnp.exp(scores - log_total[..., None])
        value_sum = value_sum + jnp.einsum('gqk,qgd->kd', round_half(probs), grad_block)
        grad_probs = jnp.einsum('qgd,kd->gqk', grad_block, value_float)
        grad_scores = round_half(scaling * probs * (grad_probs - row_dots[..., None]))
        query_block_grad = jnp.einsum('gqk,kd->qgd', grad_scores, key_float)
        key_sum = key_sum + jnp.einsum('gqk,qgd->kd', grad_scores, query_block)
        return (key_sum, value_sum), (jnp.transpose(output_block, (1, 0, 2)), query_block_grad.astype(jnp.bfloat16))

    zeroed = jnp.zeros(key_head.shape, jnp.float32)
    block_count = total_rows // block_rows
    (key_sum, value_sum), (outputs, query_grads) = lax.scan(
        visit_block, (zeroed, zeroed), jnp.arange(block_count, dtype=jnp.int32))
    outputs = outputs.reshape(total_rows, GROUP, HEAD_DIM)
    query_grads = query_grads.reshape(total_rows, GROUP, HEAD_DIM)
    return outputs, query_grads, key_sum.astype(jnp.bfloat16), value_sum.astype(jnp.bfloat16)


def reference(queries, keys, values, out_grad):
    total_rows = queries.shape[0]
    query_heads = jnp.transpose(queries.reshape(total_rows, KV_HEADS, GROUP, HEAD_DIM), (1, 0, 2, 3))
    grad_heads = jnp.transpose(out_grad.reshape(total_rows, KV_HEADS, GROUP, HEAD_DIM), (1, 0, 2, 3))
    key_heads = jnp.transpose(keys, (1, 0, 2))
    value_heads = jnp.transpose(values, (1, 0, 2))
    outputs, query_grads, key_grads, value_grads = lax.map(
        one_head, (query_heads, key_heads, value_heads, grad_heads))
    attended = jnp.transpose(outputs, (1, 0, 2, 3)).reshape(total_rows, HEADS, HEAD_DIM)
    query_grad = jnp.transpose(query_grads, (1, 0, 2, 3)).reshape(total_rows, HEADS, HEAD_DIM)
    key_grad = jnp.transpose(key_grads, (1, 0, 2))
    value_grad = jnp.transpose(value_grads, (1, 0, 2))
    return (attended, query_grad, key_grad, value_grad)
```

```python
import math

import jax
import jax.numpy as jnp
from jax import lax
from jax.experimental import pallas as pl
from jax.experimental.pallas import tpu as pltpu
from jax.sharding import Mesh, PartitionSpec as P

HEAD_DIM = 128
SCALE = HEAD_DIM ** (-0.5)
EXP2_SCALE = SCALE * math.log2(math.e)
CHIPS = ("x", "yl", "yh")
NCHIP = 16
ROWS = 128
QB = 256
KB = 512
F32 = jnp.float32
BF16 = jnp.bfloat16


def dot(a, b):
    return jnp.dot(a, b, preferred_element_type=F32)


def dot_t(a, b):
    return lax.dot_general(a, b, (((1,), (1,)), ((), ())), preferred_element_type=F32)


def attention_kernel(
    q_ref, g_ref, kva_ref, kvb_ref,
    out_ref, dq_ref, da_ref, db_ref,
    kt, vt, s_buf, p_buf, ds_buf, gn_buf, d_buf, dqt,
):
    rows = q_ref.shape[0]
    nq = rows // QB
    per = KB // ROWS
    half_chunks = NCHIP // per

    vt[HEAD_DIM:, :] = jnp.ones((vt.shape[0] - HEAD_DIM, vt.shape[1]), BF16)
    for half, ref in enumerate((kva_ref, kvb_ref)):
        @pl.loop(0, NCHIP)
        def _(b, half=half, ref=ref):
            col = pl.multiple_of((half * NCHIP + b) * ROWS, ROWS)
            kt[:, pl.ds(col, ROWS)] = jnp.transpose(ref[b, :ROWS, :])
            vt[:HEAD_DIM, pl.ds(col, ROWS)] = jnp.transpose(ref[b, ROWS:, :])

    def keys(ref, c):
        return ref[pl.ds(c * per, per), :ROWS, :].reshape(KB, HEAD_DIM)

    def vals(ref, c):
        return ref[pl.ds(c * per, per), ROWS:, :].reshape(KB, HEAD_DIM)

    for b in range(nq):
        qs = slice(b * QB, (b + 1) * QB)
        qb = q_ref[qs, :]

        top = jnp.full((8, QB), -jnp.inf, F32)
        for half, ref in enumerate((kva_ref, kvb_ref)):
            def scores(c, top, half=half, ref=ref):
                row = pl.multiple_of((half * half_chunks + c) * KB, KB)
                s = dot_t(keys(ref, c), qb)
                s_buf[pl.ds(row, KB), :] = s
                return jnp.maximum(top, jnp.max(s.reshape(KB // 8, 8, QB), axis=0))
            top = lax.fori_loop(0, half_chunks, scores, top)
        peak = jnp.max(top, axis=0, keepdims=True) * EXP2_SCALE

        def weigh(c, acc):
            row = pl.multiple_of(c * KB, KB)
            p = jnp.exp2(s_buf[pl.ds(row, KB), :] * EXP2_SCALE - peak).astype(BF16)
            p_buf[pl.ds(row, KB), qs] = p
            return acc + dot(vt[:, pl.ds(row, KB)], p)
        acc = lax.fori_loop(0, 2 * half_chunks, weigh, jnp.zeros((vt.shape[0], QB), F32))

        inv = 1.0 / acc[HEAD_DIM:HEAD_DIM + 1, :]
        out_t = acc[:HEAD_DIM, :] * inv
        out_ref[qs, :] = jnp.transpose(out_t).astype(BF16)
        inv_rows = jnp.transpose(jnp.broadcast_to(inv, (HEAD_DIM, QB)))
        gn = (g_ref[qs, :].astype(F32) * inv_rows).astype(BF16)
        gn_buf[qs, :] = gn
        gn_t = jnp.transpose(gn.astype(F32))
        d_buf[:, qs] = jnp.broadcast_to(jnp.sum(gn_t * out_t, axis=0, keepdims=True), (8, QB))

    dqt[...] = jnp.zeros_like(dqt)
    for half, (ref, dref) in enumerate(((kva_ref, da_ref), (kvb_ref, db_ref))):
        def back(c, carry, half=half, ref=ref, dref=dref):
            row = pl.multiple_of((half * half_chunks + c) * KB, KB)
            v = vals(ref, c)
            dv = dot(p_buf[pl.ds(row, KB), :], gn_buf[...])
            dref[pl.ds(c * per, per), ROWS:, :] = dv.astype(BF16).reshape(per, ROWS, HEAD_DIM)
            for b in range(nq):
                qs = slice(b * QB, (b + 1) * QB)
                dp = dot_t(v, gn_buf[qs, :])
                ds = (p_buf[pl.ds(row, KB), qs].astype(F32) * (dp - d_buf[0:1, qs])).astype(BF16)
                ds_buf[:, qs] = ds
                dqt[:, qs] += dot(kt[:, pl.ds(row, KB)], ds)
            dk = dot(ds_buf[...], q_ref[...]) * SCALE
            dref[pl.ds(c * per, per), :ROWS, :] = dk.astype(BF16).reshape(per, ROWS, HEAD_DIM)
            return carry
        lax.fori_loop(0, half_chunks, back, 0)
    for b in range(nq):
        qs = slice(b * QB, (b + 1) * QB)
        dq_ref[qs, :] = (jnp.transpose(dqt[:, qs]) * SCALE).astype(BF16)


def attention(q, g, kva, kvb):
    rows = q.shape[0]
    total = 2 * NCHIP * ROWS
    vmem = pl.BlockSpec(memory_space=pltpu.VMEM)
    return pl.pallas_call(
        attention_kernel,
        out_shape=(
            jax.ShapeDtypeStruct(q.shape, BF16),
            jax.ShapeDtypeStruct(q.shape, BF16),
            jax.ShapeDtypeStruct(kva.shape, BF16),
            jax.ShapeDtypeStruct(kvb.shape, BF16),
        ),
        in_specs=[vmem] * 4,
        out_specs=(vmem,) * 4,
        scratch_shapes=[
            pltpu.VMEM((HEAD_DIM, total), BF16),
            pltpu.VMEM((HEAD_DIM + 16, total), BF16),
            pltpu.VMEM((total, QB), F32),
            pltpu.VMEM((total, rows), BF16),
            pltpu.VMEM((KB, rows), BF16),
            pltpu.VMEM((rows, HEAD_DIM), BF16),
            pltpu.VMEM((8, rows), F32),
            pltpu.VMEM((HEAD_DIM, rows), F32),
        ],
        cost_estimate=pl.CostEstimate(
            flops=12 * rows * total * HEAD_DIM, transcendentals=rows * total, bytes_accessed=6 << 20
        ),
        compiler_params=pltpu.CompilerParams(vmem_limit_bytes=56 << 20),
    )(q, g, kva, kvb)


def swap_cores(a):
    return lax.ppermute(a, "c", [(0, 1), (1, 0)])


def exchange(a):
    return lax.all_to_all(a, CHIPS, 0, 0, tiled=True)


def on_device(queries, keys, values, out_grad):
    kv = jnp.concatenate([keys[:, 0, :], values[:, 0, :]], axis=0)
    kva = exchange(jnp.broadcast_to(kv[None], (NCHIP,) + kv.shape))
    kvb = swap_cores(kva)
    q = queries.reshape(-1, HEAD_DIM)
    g = out_grad.reshape(-1, HEAD_DIM)
    out, dq, da, db = attention(q, g, kva, kvb)
    mine = swap_cores(db)
    terms = exchange((da.astype(F32) + mine.astype(F32)).astype(BF16))
    total = jnp.sum(terms.astype(F32), axis=0).astype(BF16)
    return (
        out.reshape(queries.shape),
        dq.reshape(queries.shape),
        total[:ROWS].reshape(keys.shape),
        total[ROWS:].reshape(values.shape),
    )


def solution(mesh):
    fine = Mesh(mesh.devices.reshape(4, 2, 2, 2, 8), CHIPS + ("c", "z"))
    spec = P(CHIPS + ("c",), "z", None)
    return jax.shard_map(
        on_device,
        mesh=fine,
        in_specs=(spec,) * 4,
        out_specs=(spec,) * 4,
        check_vma=False,
    )
```

```python
import functools
import math

import jax
import jax.numpy as jnp
from jax import lax
from jax.experimental import pallas as pl
from jax.experimental.pallas import tpu as pltpu
from jax.sharding import Mesh, PartitionSpec as P

HEAD_DIM = 128
SCALE = HEAD_DIM ** (-0.5)
EXP2_SCALE = SCALE * math.log2(math.e)
CHIPS = ("x", "yl", "yh")
NCHIP = 16
ROWS = 128
QB = 256
KA = 1024
KB = 512
F32 = jnp.float32
BF16 = jnp.bfloat16


def dot(a, b):
    return jnp.dot(a, b, preferred_element_type=F32)


def dot_t(a, b):
    return lax.dot_general(a, b, (((1,), (1,)), ((), ())), preferred_element_type=F32)


def attention_kernel(q_ref, g_ref, kva_ref, kvb_ref, out_ref, dq_ref, da_ref, db_ref, *f32_scratch):
    rows = q_ref.shape[0]
    total = 2 * NCHIP * ROWS
    pl.run_scoped(
        functools.partial(
            attention_body, q_ref, g_ref, kva_ref, kvb_ref, out_ref, dq_ref, da_ref, db_ref, *f32_scratch
        ),
        pltpu.VMEM((rows, HEAD_DIM), BF16),
        pltpu.VMEM((total, HEAD_DIM), BF16),
        pltpu.VMEM((total, HEAD_DIM), BF16),
        pltpu.VMEM((HEAD_DIM, total), BF16),
        pltpu.VMEM((HEAD_DIM + 16, total), BF16),
        pltpu.VMEM((total, rows), BF16),
        pltpu.VMEM((KB, rows), BF16),
        pltpu.VMEM((KB, rows), BF16),
        pltpu.VMEM((rows, HEAD_DIM), BF16),
    )


def attention_body(
    q_ref, g_ref, kva_ref, kvb_ref,
    out_ref, dq_ref, da_ref, db_ref,
    s0, s1, acc, d_buf, dqt,
    q_all, k_all, v_all, kt, vt, p_buf, ds0, ds1, gn_buf,
):
    rows = q_ref.shape[0]
    total = k_all.shape[0]
    nq = rows // QB
    per = KB // ROWS
    chunks = total // KB

    def span(b):
        return slice(b * QB, (b + 1) * QB)

    q_all[...] = q_ref[...]
    vt[HEAD_DIM:, :] = jnp.ones((vt.shape[0] - HEAD_DIM, total), BF16)
    for half, ref in enumerate((kva_ref, kvb_ref)):
        def spread(i, carry, half=half, ref=ref):
            for j in range(4):
                b = i * 4 + j
                col = pl.multiple_of((half * NCHIP + b) * ROWS, ROWS)
                k = ref[b, :ROWS, :]
                v = ref[b, ROWS:, :]
                k_all[pl.ds(col, ROWS), :] = k
                v_all[pl.ds(col, ROWS), :] = v
                kt[:, pl.ds(col, ROWS)] = jnp.transpose(k)
                vt[:HEAD_DIM, pl.ds(col, ROWS)] = jnp.transpose(v)
            return carry
        lax.fori_loop(0, NCHIP // 4, spread, 0)

    def finish(b):
        qs = span(b)
        inv = 1.0 / acc[HEAD_DIM:HEAD_DIM + 1, :]
        out_t = acc[:HEAD_DIM, :] * inv
        out_ref[qs, :] = jnp.transpose(out_t).astype(BF16)
        inv_rows = jnp.transpose(jnp.broadcast_to(inv, (HEAD_DIM, QB)))
        gn = (g_ref[qs, :].astype(F32) * inv_rows).astype(BF16)
        gn_buf[qs, :] = gn
        gn_t = jnp.transpose(gn.astype(F32))
        d_buf[:, qs] = jnp.broadcast_to(jnp.sum(gn_t * out_t, axis=0, keepdims=True), (8, QB))

    s_bufs = (s0, s1)
    peak = None
    for stage in range(nq + 1):
        new = stage if stage < nq else None
        old = stage - 1 if stage > 0 else None
        if old is not None:
            acc[...] = jnp.zeros_like(acc)

        def forward(c, top, new=new, old=old, peak=peak):
            row = pl.multiple_of(c * KA, KA)
            if new is not None:
                s = dot_t(k_all[pl.ds(row, KA), :], q_all[span(new), :])
                s_bufs[new % 2][pl.ds(row, KA), :] = s
                top = jnp.maximum(top, jnp.max(s.reshape(KA // 8, 8, QB), axis=0))
            if old is not None:
                p = jnp.exp2(s_bufs[old % 2][pl.ds(row, KA), :] * EXP2_SCALE - peak).astype(BF16)
                p_buf[pl.ds(row, KA), span(old)] = p
                acc[...] += dot(vt[:, pl.ds(row, KA)], p)
            return top
        top = lax.fori_loop(0, total // KA, forward, jnp.full((8, QB), -jnp.inf, F32))
        if old is not None:
            finish(old)
        peak = jnp.max(top, axis=0, keepdims=True) * EXP2_SCALE

    dqt[...] = jnp.zeros_like(dqt)
    ds_bufs = (ds0, ds1)

    def score_grad(c, b):
        keys, qs = slice(c * KB, (c + 1) * KB), span(b)
        dp = dot_t(v_all[keys, :], gn_buf[qs, :])
        ds_bufs[c % 2][:, qs] = (p_buf[keys, qs].astype(F32) * (dp - d_buf[0:1, qs])).astype(BF16)

    def store(c, part, lo, value):
        ref = (da_ref, db_ref)[c * per // NCHIP]
        first = (c * per) % NCHIP + lo // ROWS
        n = value.shape[0] // ROWS
        ref[first:first + n, part * ROWS:(part + 1) * ROWS, :] = value.astype(BF16).reshape(n, ROWS, HEAD_DIM)

    def value_grad(c, lo):
        store(c, 1, lo, dot(p_buf[c * KB + lo:c * KB + lo + KB // 2, :], gn_buf[...]))

    def key_grad(c, lo):
        store(c, 0, lo, dot(ds_bufs[c % 2][lo:lo + KB // 2, :], q_all[...]) * SCALE)

    def query_grad(c, b):
        dqt[:, span(b)] += dot(kt[:, c * KB:(c + 1) * KB], ds_bufs[c % 2][:, span(b)])

    for c in range(chunks + 1):
        prior = c - 1
        for b in range(nq):
            if c < chunks:
                score_grad(c, b)
            if prior >= 0:
                if b == 0:
                    value_grad(prior, 0)
                    value_grad(prior, KB // 2)
                elif b == 1:
                    key_grad(prior, 0)
                    key_grad(prior, KB // 2)
                else:
                    query_grad(prior, 2 * b - 4)
                    query_grad(prior, 2 * b - 3)
    for b in range(nq):
        dq_ref[span(b), :] = (jnp.transpose(dqt[:, span(b)]) * SCALE).astype(BF16)


def attention(q, g, kva, kvb):
    rows = q.shape[0]
    total = 2 * NCHIP * ROWS
    vmem = pl.BlockSpec(memory_space=pltpu.VMEM)
    return pl.pallas_call(
        attention_kernel,
        out_shape=(
            jax.ShapeDtypeStruct(q.shape, BF16),
            jax.ShapeDtypeStruct(q.shape, BF16),
            jax.ShapeDtypeStruct(kva.shape, BF16),
            jax.ShapeDtypeStruct(kvb.shape, BF16),
        ),
        in_specs=[vmem] * 4,
        out_specs=(vmem,) * 4,
        scratch_shapes=[
            pltpu.VMEM((total, QB), F32),
            pltpu.VMEM((total, QB), F32),
            pltpu.VMEM((HEAD_DIM + 16, QB), F32),
            pltpu.VMEM((8, rows), F32),
            pltpu.VMEM((HEAD_DIM, rows), F32),
        ],
        cost_estimate=pl.CostEstimate(
            flops=12 * rows * total * HEAD_DIM, transcendentals=rows * total, bytes_accessed=6 << 20
        ),
        compiler_params=pltpu.CompilerParams(vmem_limit_bytes=56 << 20),
    )(q, g, kva, kvb)


def swap_cores(a):
    return lax.ppermute(a, "c", [(0, 1), (1, 0)])


def exchange(a):
    return lax.all_to_all(a, CHIPS, 0, 0, tiled=True)


def on_device(queries, keys, values, out_grad):
    kv = jnp.concatenate([keys[:, 0, :], values[:, 0, :]], axis=0)
    kva = exchange(jnp.broadcast_to(kv[None], (NCHIP,) + kv.shape))
    kvb = swap_cores(kva)
    q = queries.reshape(-1, HEAD_DIM)
    g = out_grad.reshape(-1, HEAD_DIM)
    out, dq, da, db = attention(q, g, kva, kvb)
    mine = swap_cores(db)
    terms = exchange((da.astype(F32) + mine.astype(F32)).astype(BF16))
    total = jnp.sum(terms.astype(F32), axis=0).astype(BF16)
    return (
        out.reshape(queries.shape),
        dq.reshape(queries.shape),
        total[:ROWS].reshape(keys.shape),
        total[ROWS:].reshape(values.shape),
    )


def solution(mesh):
    fine = Mesh(mesh.devices.reshape(4, 2, 2, 2, 8), CHIPS + ("c", "z"))
    spec = P(CHIPS + ("c",), "z", None)
    return jax.shard_map(
        on_device,
        mesh=fine,
        in_specs=(spec,) * 4,
        out_specs=(spec,) * 4,
        check_vma=False,
    )
```

```python
import math

import jax
import jax.numpy as jnp
from jax import lax
from jax.experimental import pallas as pl
from jax.experimental.pallas import tpu as pltpu
from jax.sharding import Mesh, PartitionSpec as P

HEAD_DIM = 128
SCALE = HEAD_DIM ** (-0.5)
EXP2_SCALE = SCALE * math.log2(math.e)
LOG2E = math.log2(math.e)
CHIPS = ("x", "yl", "yh")
NCHIP = 16
ROWS = 128
KEYS = NCHIP * ROWS
QB = 256
KB = 512
VMEM_LIMIT = 32 << 20
F32 = jnp.float32
BF16 = jnp.bfloat16


def dot(a, b):
    return jnp.dot(a, b, preferred_element_type=F32)


def dot_t(a, b):
    return lax.dot_general(a, b, (((1,), (1,)), ((), ())), preferred_element_type=F32)


def span(b):
    return slice(b * QB, (b + 1) * QB)


def as_rows(line):
    return jnp.transpose(jnp.broadcast_to(line, (HEAD_DIM, line.shape[1])))


def forward_kernel(q_ref, q2_ref, g_ref, g2_ref, kv_ref, stat_ref, own_ref, send_ref, s0, s1):
    own_rows = q_ref.shape[0]
    rows = 2 * own_rows

    def body(q_all, k_all, vt):
        q_all[:own_rows, :] = q_ref[...]
        q_all[own_rows:, :] = q2_ref[...]
        vt[HEAD_DIM:, :] = jnp.ones((vt.shape[0] - HEAD_DIM, KEYS), BF16)
        for b in range(NCHIP):
            block = slice(b * ROWS, (b + 1) * ROWS)
            k_all[block, :] = kv_ref[b, :ROWS, :]
            vt[:HEAD_DIM, block] = jnp.transpose(kv_ref[b, ROWS:, :])
        stat_ref[...] = jnp.zeros_like(stat_ref)

        def finish(b, acc, peak):
            qs = span(b)
            total = acc[HEAD_DIM:HEAD_DIM + 1, :]
            out_t = acc[:HEAD_DIM, :] * (1.0 / total)
            half, lo = divmod(b * QB, own_rows)
            local = slice(lo, lo + QB)
            grad_t = jnp.transpose((g_ref, g2_ref)[half][local, :].astype(F32))
            stat_ref[0:1, qs] = peak
            stat_ref[1:2, qs] = total
            stat_ref[2:3, qs] = jnp.sum(grad_t * out_t, axis=0, keepdims=True)
            out = jnp.transpose(out_t)
            if half == 0:
                own_ref[local, :] = out
            else:
                send_ref[local, :] = out.astype(BF16)

        s_bufs = (s0, s1)
        peak = None
        for stage in range(rows // QB + 1):
            old_peak = peak
            if stage < rows // QB:
                s = dot_t(k_all[...], q_all[span(stage), :])
                s_bufs[stage % 2][...] = s
                top = jnp.max(s.reshape(KEYS // 8, 8, QB), axis=0)
                peak = jnp.max(top, axis=0, keepdims=True) * EXP2_SCALE
            if stage > 0:
                b = stage - 1
                p = jnp.exp2(s_bufs[b % 2][...] * EXP2_SCALE - old_peak).astype(BF16)
                finish(b, dot(vt[...], p), old_peak)

    pl.run_scoped(
        body,
        pltpu.VMEM((rows, HEAD_DIM), BF16),
        pltpu.VMEM((KEYS, HEAD_DIM), BF16),
        pltpu.VMEM((HEAD_DIM + 16, KEYS), BF16),
    )


def backward_kernel(
    q_ref, q2_ref, g_ref, g2_ref, kv_ref, stat_ref, stat2_ref, own_ref, recv_ref,
    out_ref, dq_ref, send_ref, dkv_ref,
    lse, dots, dqt,
):
    own_rows = q_ref.shape[0]
    rows = 2 * own_rows
    nq = rows // QB
    per = KB // ROWS
    chunks = KEYS // KB

    def body(q_all, g_all, k_all, v_all, kt, p0, p1, ds0, ds1):
        q_all[:own_rows, :] = q_ref[...]
        q_all[own_rows:, :] = q2_ref[...]
        g_all[:own_rows, :] = g_ref[...]
        g_all[own_rows:, :] = g2_ref[...]
        for b in range(NCHIP):
            block = slice(b * ROWS, (b + 1) * ROWS)
            k = kv_ref[b, :ROWS, :]
            k_all[block, :] = k
            v_all[block, :] = kv_ref[b, ROWS:, :]
            kt[:, block] = jnp.transpose(k)

        for half in range(2):
            here = slice(half * own_rows, (half + 1) * own_rows)
            there = slice((1 - half) * own_rows, (2 - half) * own_rows)
            peak_a, peak_b = stat_ref[0:1, here], stat2_ref[0:1, there]
            peak = jnp.maximum(peak_a, peak_b)
            total_a = stat_ref[1:2, here] * jnp.exp2(peak_a - peak)
            total_b = stat2_ref[1:2, there] * jnp.exp2(peak_b - peak)
            total = total_a + total_b
            weight_a, weight_b = total_a / total, total_b / total
            lse[:, here] = jnp.broadcast_to(peak + jnp.log(total) * LOG2E, (8, own_rows))
            dots[:, here] = jnp.broadcast_to(
                weight_a * stat_ref[2:3, here] + weight_b * stat2_ref[2:3, there], (8, own_rows)
            )
            if half == 0:
                for lo in range(0, own_rows, QB):
                    local = slice(lo, lo + QB)
                    out_ref[local, :] = (
                        own_ref[local, :] * as_rows(weight_a[:, local])
                        + recv_ref[local, :].astype(F32) * as_rows(weight_b[:, local])
                    ).astype(BF16)

        dqt[...] = jnp.zeros_like(dqt)
        p_bufs, ds_bufs = (p0, p1), (ds0, ds1)

        def score_grad(c, b):
            keys, qs = slice(c * KB, (c + 1) * KB), span(b)
            s = dot_t(k_all[keys, :], q_all[qs, :])
            dp = dot_t(v_all[keys, :], g_all[qs, :])
            p = jnp.exp2(s * EXP2_SCALE - lse[0:1, qs])
            p_bufs[c % 2][:, qs] = p.astype(BF16)
            ds_bufs[c % 2][:, qs] = (p * (dp - dots[0:1, qs])).astype(BF16)

        def store(c, part, lo, value):
            first = c * per + lo // ROWS
            n = value.shape[0] // ROWS
            dkv_ref[first:first + n, part * ROWS:(part + 1) * ROWS, :] = value.astype(BF16).reshape(
                n, ROWS, HEAD_DIM
            )

        def value_grad(c, lo):
            store(c, 1, lo, dot(p_bufs[c % 2][lo:lo + KB // 2, :], g_all[...]))

        def key_grad(c, lo):
            store(c, 0, lo, dot(ds_bufs[c % 2][lo:lo + KB // 2, :], q_all[...]) * SCALE)

        def query_grad(c, b):
            dqt[:, span(b)] += dot(kt[:, c * KB:(c + 1) * KB], ds_bufs[c % 2][:, span(b)])

        for c in range(chunks + 1):
            prior = c - 1
            for b in range(nq):
                if c < chunks:
                    score_grad(c, b)
                if prior >= 0:
                    if b < 2:
                        value_grad(prior, b * (KB // 2))
                    elif b < 4:
                        key_grad(prior, (b - 2) * (KB // 2))
                    else:
                        query_grad(prior, 2 * b - 8)
                        query_grad(prior, 2 * b - 7)
        for b in range(nq):
            half, lo = divmod(b * QB, own_rows)
            (dq_ref, send_ref)[half][lo:lo + QB, :] = jnp.transpose(dqt[:, span(b)]) * SCALE

    pl.run_scoped(
        body,
        pltpu.VMEM((rows, HEAD_DIM), BF16),
        pltpu.VMEM((rows, HEAD_DIM), BF16),
        pltpu.VMEM((KEYS, HEAD_DIM), BF16),
        pltpu.VMEM((KEYS, HEAD_DIM), BF16),
        pltpu.VMEM((HEAD_DIM, KEYS), BF16),
        *[pltpu.VMEM((KB, rows), BF16) for _ in range(4)],
    )


def forward(q, q2, g, g2, kv):
    n = q.shape[0]
    vmem = pl.BlockSpec(memory_space=pltpu.VMEM)
    return pl.pallas_call(
        forward_kernel,
        out_shape=(
            jax.ShapeDtypeStruct((8, 2 * n), F32),
            jax.ShapeDtypeStruct(q.shape, F32),
            jax.ShapeDtypeStruct(q.shape, BF16),
        ),
        in_specs=[vmem] * 5,
        out_specs=(vmem,) * 3,
        scratch_shapes=[pltpu.VMEM((KEYS, QB), F32), pltpu.VMEM((KEYS, QB), F32)],
        cost_estimate=pl.CostEstimate(
            flops=8 * n * KEYS * HEAD_DIM, transcendentals=2 * n * KEYS, bytes_accessed=3 << 20
        ),
        compiler_params=pltpu.CompilerParams(vmem_limit_bytes=VMEM_LIMIT),
    )(q, q2, g, g2, kv)


def backward(q, q2, g, g2, kv, stat, stat2, own, recv):
    n = q.shape[0]
    vmem = pl.BlockSpec(memory_space=pltpu.VMEM)
    return pl.pallas_call(
        backward_kernel,
        out_shape=(
            jax.ShapeDtypeStruct(q.shape, BF16),
            jax.ShapeDtypeStruct(q.shape, F32),
            jax.ShapeDtypeStruct(q.shape, F32),
            jax.ShapeDtypeStruct(kv.shape, BF16),
        ),
        in_specs=[vmem] * 9,
        out_specs=(vmem,) * 4,
        scratch_shapes=[
            pltpu.VMEM((8, 2 * n), F32),
            pltpu.VMEM((8, 2 * n), F32),
            pltpu.VMEM((HEAD_DIM, 2 * n), F32),
        ],
        cost_estimate=pl.CostEstimate(
            flops=20 * n * KEYS * HEAD_DIM, transcendentals=2 * n * KEYS, bytes_accessed=5 << 20
        ),
        compiler_params=pltpu.CompilerParams(vmem_limit_bytes=VMEM_LIMIT),
    )(q, q2, g, g2, kv, stat, stat2, own, recv)


def swap_cores(a):
    return lax.ppermute(a, "c", [(0, 1), (1, 0)])


def exchange(a):
    return lax.all_to_all(a, CHIPS, 0, 0, tiled=True)


def on_device(queries, keys, values, out_grad):
    q = queries.reshape(-1, HEAD_DIM)
    g = out_grad.reshape(-1, HEAD_DIM)
    q2, g2 = swap_cores(q), swap_cores(g)
    kv = jnp.concatenate([keys[:, 0, :], values[:, 0, :]], axis=0)
    kv = exchange(jnp.broadcast_to(kv[None], (NCHIP,) + kv.shape))
    stat, own, send = forward(q, q2, g, g2, kv)
    stat2, recv = swap_cores(stat), swap_cores(send)
    out, dq, dq_send, dkv = backward(q, q2, g, g2, kv, stat, stat2, own, recv)
    terms = exchange(dkv)
    dq = (dq + swap_cores(dq_send)).astype(BF16)
    total = jnp.sum(terms.astype(F32), axis=0).astype(BF16)
    return (
        out.reshape(queries.shape),
        dq.reshape(queries.shape),
        total[:ROWS].reshape(keys.shape),
        total[ROWS:].reshape(values.shape),
    )


def solution(mesh):
    fine = Mesh(mesh.devices.reshape(4, 2, 2, 2, 8), CHIPS + ("c", "z"))
    spec = P(CHIPS + ("c",), "z", None)
    return jax.shard_map(
        on_device,
        mesh=fine,
        in_specs=(spec,) * 4,
        out_specs=(spec,) * 4,
        check_vma=False,
    )
```

```python
import math

import jax
import jax.numpy as jnp
from jax import lax
from jax.experimental import pallas as pl
from jax.experimental.pallas import tpu as pltpu
from jax.sharding import Mesh, PartitionSpec as P


HEAD_DIM = 128
SCALE = HEAD_DIM ** (-0.5)
EXP2_SCALE = SCALE * math.log2(math.e)
LOG2E = math.log2(math.e)
CHIPS = ("x", "yl", "yh")
NCHIP = 16
ROWS = 128
KEYS = NCHIP * ROWS
QB = 256
KF = 512
KB = 512
VMEM_LIMIT = 32 << 20
F32 = jnp.float32
BF16 = jnp.bfloat16


def dot(a, b):
    return jnp.dot(a, b, preferred_element_type=F32)


def dot_t(a, b):
    return lax.dot_general(a, b, (((1,), (1,)), ((), ())), preferred_element_type=F32)


def span(b):
    return slice(b * QB, (b + 1) * QB)


def as_rows(line):
    return jnp.transpose(jnp.broadcast_to(line, (HEAD_DIM, line.shape[1])))


def forward_kernel(q_ref, q2_ref, g_ref, g2_ref, kv_ref, stat_ref, own_ref, send_ref, s0, s1):
    own_rows = q_ref.shape[0]
    rows = 2 * own_rows

    def body(q_all, k_all, vt):
        q_all[:own_rows, :] = q_ref[...]
        q_all[own_rows:, :] = q2_ref[...]
        vt[HEAD_DIM:, :] = jnp.ones((vt.shape[0] - HEAD_DIM, KEYS), BF16)
        for b in range(NCHIP):
            block = slice(b * ROWS, (b + 1) * ROWS)
            k_all[block, :] = kv_ref[b, :ROWS, :]
            vt[:HEAD_DIM, block] = jnp.transpose(kv_ref[b, ROWS:, :])
        stat_ref[...] = jnp.zeros_like(stat_ref)

        def finish(b, acc, peak):
            qs = span(b)
            total = acc[HEAD_DIM:HEAD_DIM + 1, :]
            out_t = acc[:HEAD_DIM, :] * (1.0 / total)
            half, lo = divmod(b * QB, own_rows)
            local = slice(lo, lo + QB)
            grad_t = jnp.transpose((g_ref, g2_ref)[half][local, :].astype(F32))
            stat_ref[0:1, qs] = peak
            stat_ref[1:2, qs] = total
            stat_ref[2:3, qs] = jnp.sum(grad_t * out_t, axis=0, keepdims=True)
            out = jnp.transpose(out_t)
            if half == 0:
                own_ref[local, :] = out
            else:
                send_ref[local, :] = out.astype(BF16)

        s_bufs = (s0, s1)
        peak = None
        for stage in range(rows // QB + 1):
            old_peak = peak
            top = None
            acc = None
            for lo in range(0, KEYS, KF):
                if stage < rows // QB:
                    s = dot_t(k_all[lo:lo + KF, :], q_all[span(stage), :])
                    s_bufs[stage % 2][lo:lo + KF, :] = s
                    part = jnp.max(s.reshape(KF // 8, 8, QB), axis=0)
                    top = part if top is None else jnp.maximum(top, part)
                if stage > 0:
                    b = stage - 1
                    p = jnp.exp2(s_bufs[b % 2][lo:lo + KF, :] * EXP2_SCALE - old_peak).astype(BF16)
                    term = dot(vt[:, lo:lo + KF], p)
                    acc = term if acc is None else acc + term
            if stage < rows // QB:
                peak = jnp.max(top, axis=0, keepdims=True) * EXP2_SCALE
            if stage > 0:
                finish(stage - 1, acc, old_peak)

    pl.run_scoped(
        body,
        pltpu.VMEM((rows, HEAD_DIM), BF16),
        pltpu.VMEM((KEYS, HEAD_DIM), BF16),
        pltpu.VMEM((HEAD_DIM + 16, KEYS), BF16),
    )


def backward_kernel(
    q_ref, q2_ref, g_ref, g2_ref, kv_ref, stat_ref, stat2_ref, own_ref, recv_ref,
    out_ref, dq_ref, send_ref, dkv_ref,
    lse, dots, dqt,
):
    own_rows = q_ref.shape[0]
    rows = 2 * own_rows
    nq = rows // QB
    per = KB // ROWS
    chunks = KEYS // KB

    def body(q_all, g_all, k_all, v_all, kt, p0, p1, ds0, ds1):
        q_all[:own_rows, :] = q_ref[...]
        q_all[own_rows:, :] = q2_ref[...]
        g_all[:own_rows, :] = g_ref[...]
        g_all[own_rows:, :] = g2_ref[...]
        for b in range(NCHIP):
            block = slice(b * ROWS, (b + 1) * ROWS)
            k = kv_ref[b, :ROWS, :]
            k_all[block, :] = k
            v_all[block, :] = kv_ref[b, ROWS:, :]
            kt[:, block] = jnp.transpose(k)

        for half in range(2):
            here = slice(half * own_rows, (half + 1) * own_rows)
            there = slice((1 - half) * own_rows, (2 - half) * own_rows)
            peak_a, peak_b = stat_ref[0:1, here], stat2_ref[0:1, there]
            peak = jnp.maximum(peak_a, peak_b)
            total_a = stat_ref[1:2, here] * jnp.exp2(peak_a - peak)
            total_b = stat2_ref[1:2, there] * jnp.exp2(peak_b - peak)
            total = total_a + total_b
            weight_a, weight_b = total_a / total, total_b / total
            lse[:, here] = jnp.broadcast_to(peak + jnp.log(total) * LOG2E, (8, own_rows))
            dots[:, here] = jnp.broadcast_to(
                weight_a * stat_ref[2:3, here] + weight_b * stat2_ref[2:3, there], (8, own_rows)
            )
            if half == 0:
                for lo in range(0, own_rows, QB):
                    local = slice(lo, lo + QB)
                    out_ref[local, :] = (
                        own_ref[local, :] * as_rows(weight_a[:, local])
                        + recv_ref[local, :].astype(F32) * as_rows(weight_b[:, local])
                    ).astype(BF16)

        dqt[...] = jnp.zeros_like(dqt)
        p_bufs, ds_bufs = (p0, p1), (ds0, ds1)

        def score_grad(c, b):
            keys, qs = slice(c * KB, (c + 1) * KB), span(b)
            s = dot_t(k_all[keys, :], q_all[qs, :])
            dp = dot_t(v_all[keys, :], g_all[qs, :])
            p = jnp.exp2(s * EXP2_SCALE - lse[0:1, qs])
            p_bufs[c % 2][:, qs] = p.astype(BF16)
            ds_bufs[c % 2][:, qs] = (p * (dp - dots[0:1, qs])).astype(BF16)

        def store(c, part, lo, value):
            first = c * per + lo // ROWS
            n = value.shape[0] // ROWS
            dkv_ref[first:first + n, part * ROWS:(part + 1) * ROWS, :] = value.astype(BF16).reshape(
                n, ROWS, HEAD_DIM
            )

        def value_grad(c, lo):
            store(c, 1, lo, dot(p_bufs[c % 2][lo:lo + KB // 2, :], g_all[...]))

        def key_grad(c, lo):
            store(c, 0, lo, dot(ds_bufs[c % 2][lo:lo + KB // 2, :], q_all[...]) * SCALE)

        def query_grad(c, b):
            dqt[:, span(b)] += dot(kt[:, c * KB:(c + 1) * KB], ds_bufs[c % 2][:, span(b)])

        for c in range(chunks + 1):
            prior = c - 1
            for b in range(nq):
                if c < chunks:
                    score_grad(c, b)
                if prior >= 0:
                    if b < 2:
                        value_grad(prior, b * (KB // 2))
                    elif b < 4:
                        key_grad(prior, (b - 2) * (KB // 2))
                    else:
                        query_grad(prior, 2 * b - 8)
                        query_grad(prior, 2 * b - 7)
        for b in range(nq):
            half, lo = divmod(b * QB, own_rows)
            (dq_ref, send_ref)[half][lo:lo + QB, :] = jnp.transpose(dqt[:, span(b)]) * SCALE

    pl.run_scoped(
        body,
        pltpu.VMEM((rows, HEAD_DIM), BF16),
        pltpu.VMEM((rows, HEAD_DIM), BF16),
        pltpu.VMEM((KEYS, HEAD_DIM), BF16),
        pltpu.VMEM((KEYS, HEAD_DIM), BF16),
        pltpu.VMEM((HEAD_DIM, KEYS), BF16),
        *[pltpu.VMEM((KB, rows), BF16) for _ in range(4)],
    )


def forward(q, q2, g, g2, kv):
    n = q.shape[0]
    vmem = pl.BlockSpec(memory_space=pltpu.VMEM)
    return pl.pallas_call(
        forward_kernel,
        out_shape=(
            jax.ShapeDtypeStruct((8, 2 * n), F32),
            jax.ShapeDtypeStruct(q.shape, F32),
            jax.ShapeDtypeStruct(q.shape, BF16),
        ),
        in_specs=[vmem] * 5,
        out_specs=(vmem,) * 3,
        scratch_shapes=[pltpu.VMEM((KEYS, QB), F32), pltpu.VMEM((KEYS, QB), F32)],
        cost_estimate=pl.CostEstimate(
            flops=8 * n * KEYS * HEAD_DIM, transcendentals=2 * n * KEYS, bytes_accessed=3 << 20
        ),
        compiler_params=pltpu.CompilerParams(vmem_limit_bytes=VMEM_LIMIT),
    )(q, q2, g, g2, kv)


def backward(q, q2, g, g2, kv, stat, stat2, own, recv):
    n = q.shape[0]
    vmem = pl.BlockSpec(memory_space=pltpu.VMEM)
    return pl.pallas_call(
        backward_kernel,
        out_shape=(
            jax.ShapeDtypeStruct(q.shape, BF16),
            jax.ShapeDtypeStruct(q.shape, F32),
            jax.ShapeDtypeStruct(q.shape, F32),
            jax.ShapeDtypeStruct(kv.shape, BF16),
        ),
        in_specs=[vmem] * 9,
        out_specs=(vmem,) * 4,
        scratch_shapes=[
            pltpu.VMEM((8, 2 * n), F32),
            pltpu.VMEM((8, 2 * n), F32),
            pltpu.VMEM((HEAD_DIM, 2 * n), F32),
        ],
        cost_estimate=pl.CostEstimate(
            flops=20 * n * KEYS * HEAD_DIM, transcendentals=2 * n * KEYS, bytes_accessed=5 << 20
        ),
        compiler_params=pltpu.CompilerParams(vmem_limit_bytes=VMEM_LIMIT),
    )(q, q2, g, g2, kv, stat, stat2, own, recv)


def swap_cores(a):
    return lax.ppermute(a, "c", [(0, 1), (1, 0)])


def exchange(a):
    return lax.all_to_all(a, CHIPS, 0, 0, tiled=True)


def step(queries, keys, values, out_grad):
    q = queries.reshape(-1, HEAD_DIM)
    g = out_grad.reshape(-1, HEAD_DIM)
    q2, g2 = swap_cores(q), swap_cores(g)
    kv = jnp.concatenate([keys[:, 0, :], values[:, 0, :]], axis=0)
    kv, q2, g2 = lax.optimization_barrier((jnp.broadcast_to(kv[None], (NCHIP,) + kv.shape), q2, g2))
    kv = exchange(kv)
    stat, own, send = forward(q, q2, g, g2, kv)
    stat2, recv = swap_cores(stat), swap_cores(send)
    out, dq, dq_send, dkv = backward(q, q2, g, g2, kv, stat, stat2, own, recv)
    dq_recv = swap_cores(dq_send)
    terms = exchange(dkv)
    dq = (dq + dq_recv).astype(BF16)
    total = jnp.sum(terms.astype(F32), axis=0).astype(BF16)
    return (
        out.reshape(queries.shape),
        dq.reshape(queries.shape),
        total[:ROWS].reshape(keys.shape),
        total[ROWS:].reshape(values.shape),
    )


def solution(mesh):
    fine = Mesh(mesh.devices.reshape(4, 2, 2, 2, 8), CHIPS + ("c", "z"))
    spec = P(CHIPS + ("c",), "z", None)
    return jax.shard_map(
        step,
        mesh=fine,
        in_specs=(spec,) * 4,
        out_specs=(spec,) * 4,
        check_vma=False,
    )
```

```python
import math

import jax
import jax.numpy as jnp
from jax import lax
from jax.experimental import pallas as pl
from jax.experimental.pallas import tpu as pltpu
from jax.sharding import Mesh, PartitionSpec as P


HEAD_DIM = 128
SCALE = HEAD_DIM ** (-0.5)
EXP2_SCALE = SCALE * math.log2(math.e)
LOG2E = math.log2(math.e)
CHIPS = ("x", "yl", "yh")
NCHIP = 16
ROWS = 128
KEYS = NCHIP * ROWS
QB = 256
KF = 512
KB = 512
VMEM_LIMIT = 32 << 20
F32 = jnp.float32
BF16 = jnp.bfloat16


def dot(a, b):
    return jnp.dot(a, b, preferred_element_type=F32)


def dot_t(a, b):
    return lax.dot_general(a, b, (((1,), (1,)), ((), ())), preferred_element_type=F32)


def span(b):
    return slice(b * QB, (b + 1) * QB)


def forward_kernel(q_ref, q2_ref, g_ref, g2_ref, kv_ref, stat_ref, half_ref, s0, s1):
    own_rows = q_ref.shape[0]
    rows = 2 * own_rows

    def body(q_all, k_all, vt):
        q_all[:own_rows, :] = q_ref[...]
        q_all[own_rows:, :] = q2_ref[...]
        vt[HEAD_DIM:, :] = jnp.ones((vt.shape[0] - HEAD_DIM, KEYS), BF16)
        for b in range(NCHIP):
            block = slice(b * ROWS, (b + 1) * ROWS)
            k_all[block, :] = kv_ref[b, :ROWS, :]
            vt[:HEAD_DIM, block] = jnp.transpose(kv_ref[b, ROWS:, :])
        stat_ref[...] = jnp.zeros_like(stat_ref)

        def finish(b, acc, peak):
            qs = span(b)
            total = acc[HEAD_DIM:HEAD_DIM + 1, :]
            out_t = acc[:HEAD_DIM, :] * (1.0 / total)
            half, lo = divmod(b * QB, own_rows)
            local = slice(lo, lo + QB)
            grad_t = jnp.transpose((g_ref, g2_ref)[half][local, :].astype(F32))
            stat_ref[0:1, qs] = peak
            stat_ref[1:2, qs] = total
            stat_ref[2:3, qs] = jnp.sum(grad_t * out_t, axis=0, keepdims=True)
            half_ref[:, qs] = out_t

        s_bufs = (s0, s1)
        peak = None
        for stage in range(rows // QB + 1):
            old_peak = peak
            top = None
            acc = None
            for lo in range(0, KEYS, KF):
                if stage < rows // QB:
                    s = dot_t(k_all[lo:lo + KF, :], q_all[span(stage), :])
                    s_bufs[stage % 2][lo:lo + KF, :] = s
                    part = jnp.max(s.reshape(KF // 8, 8, QB), axis=0)
                    top = part if top is None else jnp.maximum(top, part)
                if stage > 0:
                    b = stage - 1
                    p = jnp.exp2(s_bufs[b % 2][lo:lo + KF, :] * EXP2_SCALE - old_peak).astype(BF16)
                    term = dot(vt[:, lo:lo + KF], p)
                    acc = term if acc is None else acc + term
            if stage < rows // QB:
                peak = jnp.max(top, axis=0, keepdims=True) * EXP2_SCALE
            if stage > 0:
                finish(stage - 1, acc, old_peak)

    pl.run_scoped(
        body,
        pltpu.VMEM((rows, HEAD_DIM), BF16),
        pltpu.VMEM((KEYS, HEAD_DIM), BF16),
        pltpu.VMEM((HEAD_DIM + 16, KEYS), BF16),
    )


def backward_kernel(
    q_ref, q2_ref, g_ref, g2_ref, kv_ref, stat_ref, stat2_ref, half_ref,
    keep_ref, send_ref, dkv_ref,
    lse, dots, dqt,
):
    own_rows = q_ref.shape[0]
    rows = 2 * own_rows
    nq = rows // QB
    per = KB // ROWS
    chunks = KEYS // KB

    def body(q_all, g_all, k_all, v_all, kt, p0, p1, ds0, ds1):
        q_all[:own_rows, :] = q_ref[...]
        q_all[own_rows:, :] = q2_ref[...]
        g_all[:own_rows, :] = g_ref[...]
        g_all[own_rows:, :] = g2_ref[...]
        for b in range(NCHIP):
            block = slice(b * ROWS, (b + 1) * ROWS)
            k = kv_ref[b, :ROWS, :]
            k_all[block, :] = k
            v_all[block, :] = kv_ref[b, ROWS:, :]
            kt[:, block] = jnp.transpose(k)

        for half in range(2):
            here = slice(half * own_rows, (half + 1) * own_rows)
            there = slice((1 - half) * own_rows, (2 - half) * own_rows)
            peak_a, peak_b = stat_ref[0:1, here], stat2_ref[0:1, there]
            peak = jnp.maximum(peak_a, peak_b)
            total_a = stat_ref[1:2, here] * jnp.exp2(peak_a - peak)
            total_b = stat2_ref[1:2, there] * jnp.exp2(peak_b - peak)
            total = total_a + total_b
            weight_a = total_a / total
            lse[:, here] = jnp.broadcast_to(peak + jnp.log(total) * LOG2E, (8, own_rows))
            dots[:, here] = jnp.broadcast_to(
                weight_a * stat_ref[2:3, here] + total_b / total * stat2_ref[2:3, there], (8, own_rows)
            )
            for lo in range(0, own_rows, QB):
                at = half * own_rows + lo
                (keep_ref, send_ref)[half][lo:lo + QB, :] = jnp.transpose(
                    half_ref[:, at:at + QB] * weight_a[:, lo:lo + QB]
                )

        dqt[...] = jnp.zeros_like(dqt)
        p_bufs, ds_bufs = (p0, p1), (ds0, ds1)

        def score_grad(c, b):
            keys, qs = slice(c * KB, (c + 1) * KB), span(b)
            s = dot_t(k_all[keys, :], q_all[qs, :])
            dp = dot_t(v_all[keys, :], g_all[qs, :])
            p = jnp.exp2(s * EXP2_SCALE - lse[0:1, qs])
            p_bufs[c % 2][:, qs] = p.astype(BF16)
            ds_bufs[c % 2][:, qs] = (p * (dp - dots[0:1, qs])).astype(BF16)

        def store(c, part, lo, value):
            first = c * per + lo // ROWS
            n = value.shape[0] // ROWS
            dkv_ref[first:first + n, part * ROWS:(part + 1) * ROWS, :] = value.astype(BF16).reshape(
                n, ROWS, HEAD_DIM
            )

        def value_grad(c, lo):
            store(c, 1, lo, dot(p_bufs[c % 2][lo:lo + KB // 2, :], g_all[...]))

        def key_grad(c, lo):
            store(c, 0, lo, dot(ds_bufs[c % 2][lo:lo + KB // 2, :], q_all[...]) * SCALE)

        def query_grad(c, b):
            dqt[:, span(b)] += dot(kt[:, c * KB:(c + 1) * KB], ds_bufs[c % 2][:, span(b)])

        for c in range(chunks + 1):
            prior = c - 1
            for b in range(nq):
                if c < chunks:
                    score_grad(c, b)
                if prior >= 0:
                    if b < 2:
                        value_grad(prior, b * (KB // 2))
                    elif b < 4:
                        key_grad(prior, (b - 2) * (KB // 2))
                    else:
                        query_grad(prior, 2 * b - 8)
                        query_grad(prior, 2 * b - 7)
        for b in range(nq):
            half, lo = divmod(b * QB, own_rows)
            at = own_rows + lo
            (keep_ref, send_ref)[half][at:at + QB, :] = jnp.transpose(dqt[:, span(b)]) * SCALE

    pl.run_scoped(
        body,
        pltpu.VMEM((rows, HEAD_DIM), BF16),
        pltpu.VMEM((rows, HEAD_DIM), BF16),
        pltpu.VMEM((KEYS, HEAD_DIM), BF16),
        pltpu.VMEM((KEYS, HEAD_DIM), BF16),
        pltpu.VMEM((HEAD_DIM, KEYS), BF16),
        *[pltpu.VMEM((KB, rows), BF16) for _ in range(4)],
    )


def forward(q, q2, g, g2, kv):
    n = q.shape[0]
    vmem = pl.BlockSpec(memory_space=pltpu.VMEM)
    return pl.pallas_call(
        forward_kernel,
        out_shape=(
            jax.ShapeDtypeStruct((8, 2 * n), F32),
            jax.ShapeDtypeStruct((HEAD_DIM, 2 * n), F32),
        ),
        in_specs=[vmem] * 5,
        out_specs=(vmem,) * 2,
        scratch_shapes=[pltpu.VMEM((KEYS, QB), F32), pltpu.VMEM((KEYS, QB), F32)],
        cost_estimate=pl.CostEstimate(
            flops=8 * n * KEYS * HEAD_DIM, transcendentals=2 * n * KEYS, bytes_accessed=3 << 20
        ),
        compiler_params=pltpu.CompilerParams(vmem_limit_bytes=VMEM_LIMIT),
    )(q, q2, g, g2, kv)


def backward(q, q2, g, g2, kv, stat, stat2, half):
    n = q.shape[0]
    vmem = pl.BlockSpec(memory_space=pltpu.VMEM)
    return pl.pallas_call(
        backward_kernel,
        out_shape=(
            jax.ShapeDtypeStruct((2 * n, HEAD_DIM), F32),
            jax.ShapeDtypeStruct((2 * n, HEAD_DIM), F32),
            jax.ShapeDtypeStruct(kv.shape, BF16),
        ),
        in_specs=[vmem] * 8,
        out_specs=(vmem,) * 3,
        scratch_shapes=[
            pltpu.VMEM((8, 2 * n), F32),
            pltpu.VMEM((8, 2 * n), F32),
            pltpu.VMEM((HEAD_DIM, 2 * n), F32),
        ],
        cost_estimate=pl.CostEstimate(
            flops=20 * n * KEYS * HEAD_DIM, transcendentals=2 * n * KEYS, bytes_accessed=5 << 20
        ),
        compiler_params=pltpu.CompilerParams(vmem_limit_bytes=VMEM_LIMIT),
    )(q, q2, g, g2, kv, stat, stat2, half)


def join_kernel(keep_ref, recv_ref, total_ref, out_ref, dq_ref, dk_ref, dv_ref):
    n = out_ref.shape[0]
    out_ref[...] = (keep_ref[:n, :] + recv_ref[:n, :]).astype(BF16)
    dq_ref[...] = (keep_ref[n:, :] + recv_ref[n:, :]).astype(BF16)
    dk_ref[...] = total_ref[:ROWS, :]
    dv_ref[...] = total_ref[ROWS:, :]


def join(keep, recv, total):
    n = keep.shape[0] // 2
    vmem = pl.BlockSpec(memory_space=pltpu.VMEM)
    return pl.pallas_call(
        join_kernel,
        out_shape=tuple(jax.ShapeDtypeStruct((m, HEAD_DIM), BF16) for m in (n, n, ROWS, ROWS)),
        in_specs=[vmem] * 3,
        out_specs=(vmem,) * 4,
        compiler_params=pltpu.CompilerParams(vmem_limit_bytes=8 << 20),
    )(keep, recv, total)


def swap_cores(a):
    return lax.ppermute(a, "c", [(0, 1), (1, 0)])


def exchange(a):
    return lax.all_to_all(a, CHIPS, 0, 0, tiled=True)


def step(queries, keys, values, out_grad):
    q = queries.reshape(-1, HEAD_DIM)
    g = out_grad.reshape(-1, HEAD_DIM)
    q2, g2 = swap_cores(q), swap_cores(g)
    kv = jnp.concatenate([keys[:, 0, :], values[:, 0, :]], axis=0)
    kv, q2, g2 = lax.optimization_barrier((jnp.broadcast_to(kv[None], (NCHIP,) + kv.shape), q2, g2))
    kv = exchange(kv)
    stat, half = forward(q, q2, g, g2, kv)
    keep, send, dkv = backward(q, q2, g, g2, kv, stat, swap_cores(stat), half)
    recv = swap_cores(send)
    terms = exchange(dkv)
    total = jnp.sum(terms.astype(F32), axis=0).astype(BF16)
    out, dq, dk, dv = join(keep, recv, total)
    return (
        out.reshape(queries.shape),
        dq.reshape(queries.shape),
        dk.reshape(keys.shape),
        dv.reshape(values.shape),
    )


def solution(mesh):
    fine = Mesh(mesh.devices.reshape(4, 2, 2, 2, 8), CHIPS + ("c", "z"))
    spec = P(CHIPS + ("c",), "z", None)
    return jax.shard_map(
        step,
        mesh=fine,
        in_specs=(spec,) * 4,
        out_specs=(spec,) * 4,
        check_vma=False,
    )
```

```python
import math

import jax
import jax.numpy as jnp
from jax import lax
from jax.experimental import pallas as pl
from jax.experimental.pallas import tpu as pltpu
from jax.sharding import Mesh, PartitionSpec as P


HEAD_DIM = 128
SCALE = HEAD_DIM ** (-0.5)
EXP2_SCALE = SCALE * math.log2(math.e)
LOG2E = math.log2(math.e)
CHIPS = ("x", "yl", "yh")
NCHIP = 16
ROWS = 128
KEYS = NCHIP * ROWS
QB = 256
KF = 512
KB = 512
VMEM_LIMIT = 32 << 20
F32 = jnp.float32
BF16 = jnp.bfloat16


def dot(a, b):
    return jnp.dot(a, b, preferred_element_type=F32)


def dot_t(a, b):
    return lax.dot_general(a, b, (((1,), (1,)), ((), ())), preferred_element_type=F32)


def span(b):
    return slice(b * QB, (b + 1) * QB)


def forward_kernel(q_ref, q2_ref, g_ref, g2_ref, kv_ref, stat_ref, half_ref, s0, s1):
    own_rows = q_ref.shape[0]
    rows = 2 * own_rows

    def body(q_all, k_all, vt):
        q_all[:own_rows, :] = q_ref[...]
        q_all[own_rows:, :] = q2_ref[...]
        vt[HEAD_DIM:, :] = jnp.ones((vt.shape[0] - HEAD_DIM, KEYS), BF16)
        for b in range(NCHIP):
            block = slice(b * ROWS, (b + 1) * ROWS)
            k_all[block, :] = kv_ref[b, :ROWS, :]
            vt[:HEAD_DIM, block] = jnp.transpose(kv_ref[b, ROWS:, :])
        stat_ref[...] = jnp.zeros_like(stat_ref)

        def finish(b, acc, peak):
            qs = span(b)
            total = acc[HEAD_DIM:HEAD_DIM + 1, :]
            out_t = acc[:HEAD_DIM, :] * (1.0 / total)
            half, lo = divmod(b * QB, own_rows)
            local = slice(lo, lo + QB)
            grad_t = jnp.transpose((g_ref, g2_ref)[half][local, :].astype(F32))
            stat_ref[0:1, qs] = peak
            stat_ref[1:2, qs] = total
            stat_ref[2:3, qs] = jnp.sum(grad_t * out_t, axis=0, keepdims=True)
            half_ref[:, qs] = out_t

        s_bufs = (s0, s1)
        peak = None
        for stage in range(rows // QB + 1):
            old_peak = peak
            top = None
            acc = None
            for lo in range(0, KEYS, KF):
                if stage < rows // QB:
                    s = dot_t(k_all[lo:lo + KF, :], q_all[span(stage), :])
                    s_bufs[stage % 2][lo:lo + KF, :] = s
                    part = jnp.max(s.reshape(KF // 8, 8, QB), axis=0)
                    top = part if top is None else jnp.maximum(top, part)
                if stage > 0:
                    b = stage - 1
                    p = jnp.exp2(s_bufs[b % 2][lo:lo + KF, :] * EXP2_SCALE - old_peak).astype(BF16)
                    term = dot(vt[:, lo:lo + KF], p)
                    acc = term if acc is None else acc + term
            if stage < rows // QB:
                peak = jnp.max(top, axis=0, keepdims=True) * EXP2_SCALE
            if stage > 0:
                finish(stage - 1, acc, old_peak)

    pl.run_scoped(
        body,
        pltpu.VMEM((rows, HEAD_DIM), BF16),
        pltpu.VMEM((KEYS, HEAD_DIM), BF16),
        pltpu.VMEM((HEAD_DIM + 16, KEYS), BF16),
    )


def backward_kernel(
    q_ref, q2_ref, g_ref, g2_ref, kv_ref, stat_ref, stat2_ref, half_ref,
    keep_ref, send_ref, dkv_ref,
    lse, dots, dqt,
):
    own_rows = q_ref.shape[0]
    rows = 2 * own_rows
    nq = rows // QB
    per = KB // ROWS
    chunks = KEYS // KB

    def body(q_all, g_all, k_all, v_all, kt, p0, p1, ds0, ds1):
        q_all[:own_rows, :] = q_ref[...]
        q_all[own_rows:, :] = q2_ref[...]
        g_all[:own_rows, :] = g_ref[...]
        g_all[own_rows:, :] = g2_ref[...]
        for b in range(NCHIP):
            block = slice(b * ROWS, (b + 1) * ROWS)
            k = kv_ref[b, :ROWS, :]
            k_all[block, :] = k
            v_all[block, :] = kv_ref[b, ROWS:, :]
            kt[:, block] = jnp.transpose(k)

        for half in range(2):
            here = slice(half * own_rows, (half + 1) * own_rows)
            there = slice((1 - half) * own_rows, (2 - half) * own_rows)
            peak_a, peak_b = stat_ref[0:1, here], stat2_ref[0:1, there]
            peak = jnp.maximum(peak_a, peak_b)
            total_a = stat_ref[1:2, here] * jnp.exp2(peak_a - peak)
            total_b = stat2_ref[1:2, there] * jnp.exp2(peak_b - peak)
            total = total_a + total_b
            weight_a = total_a / total
            lse[:, here] = jnp.broadcast_to(peak + jnp.log(total) * LOG2E, (8, own_rows))
            dots[:, here] = jnp.broadcast_to(
                weight_a * stat_ref[2:3, here] + total_b / total * stat2_ref[2:3, there], (8, own_rows)
            )
            for lo in range(0, own_rows, QB):
                at = half * own_rows + lo
                (keep_ref, send_ref)[half][lo:lo + QB, :] = jnp.transpose(
                    half_ref[:, at:at + QB] * weight_a[:, lo:lo + QB]
                )

        dqt[...] = jnp.zeros_like(dqt)
        p_bufs, ds_bufs = (p0, p1), (ds0, ds1)

        def score_grad(c, b):
            keys, qs = slice(c * KB, (c + 1) * KB), span(b)
            s = dot_t(k_all[keys, :], q_all[qs, :])
            dp = dot_t(v_all[keys, :], g_all[qs, :])
            p = jnp.exp2(s * EXP2_SCALE - lse[0:1, qs])
            p_bufs[c % 2][:, qs] = p.astype(BF16)
            ds_bufs[c % 2][:, qs] = (p * (dp - dots[0:1, qs])).astype(BF16)

        def store(c, part, lo, value):
            first = c * per + lo // ROWS
            n = value.shape[0] // ROWS
            dkv_ref[first:first + n, part * ROWS:(part + 1) * ROWS, :] = value.astype(BF16).reshape(
                n, ROWS, HEAD_DIM
            )

        def value_grad(c, lo):
            store(c, 1, lo, dot(p_bufs[c % 2][lo:lo + KB // 2, :], g_all[...]))

        def key_grad(c, lo):
            store(c, 0, lo, dot(ds_bufs[c % 2][lo:lo + KB // 2, :], q_all[...]) * SCALE)

        def query_grad(c, b):
            dqt[:, span(b)] += dot(kt[:, c * KB:(c + 1) * KB], ds_bufs[c % 2][:, span(b)])

        for c in range(chunks + 1):
            prior = c - 1
            for b in range(nq):
                if c < chunks:
                    score_grad(c, b)
                if prior >= 0:
                    if b < 2:
                        value_grad(prior, b * (KB // 2))
                    elif b < 4:
                        key_grad(prior, (b - 2) * (KB // 2))
                    else:
                        query_grad(prior, 2 * b - 8)
                        query_grad(prior, 2 * b - 7)
        for b in range(nq):
            half, lo = divmod(b * QB, own_rows)
            at = own_rows + lo
            (keep_ref, send_ref)[half][at:at + QB, :] = jnp.transpose(dqt[:, span(b)]) * SCALE

    pl.run_scoped(
        body,
        pltpu.VMEM((rows, HEAD_DIM), BF16),
        pltpu.VMEM((rows, HEAD_DIM), BF16),
        pltpu.VMEM((KEYS, HEAD_DIM), BF16),
        pltpu.VMEM((KEYS, HEAD_DIM), BF16),
        pltpu.VMEM((HEAD_DIM, KEYS), BF16),
        *[pltpu.VMEM((KB, rows), BF16) for _ in range(4)],
    )


def forward(q, q2, g, g2, kv):
    n = q.shape[0]
    vmem = pl.BlockSpec(memory_space=pltpu.VMEM)
    return pl.pallas_call(
        forward_kernel,
        out_shape=(
            jax.ShapeDtypeStruct((8, 2 * n), F32),
            jax.ShapeDtypeStruct((HEAD_DIM, 2 * n), F32),
        ),
        in_specs=[vmem] * 5,
        out_specs=(vmem,) * 2,
        scratch_shapes=[pltpu.VMEM((KEYS, QB), F32), pltpu.VMEM((KEYS, QB), F32)],
        cost_estimate=pl.CostEstimate(
            flops=8 * n * KEYS * HEAD_DIM, transcendentals=2 * n * KEYS, bytes_accessed=3 << 20
        ),
        compiler_params=pltpu.CompilerParams(vmem_limit_bytes=VMEM_LIMIT),
    )(q, q2, g, g2, kv)


def backward(q, q2, g, g2, kv, stat, stat2, half):
    n = q.shape[0]
    vmem = pl.BlockSpec(memory_space=pltpu.VMEM)
    return pl.pallas_call(
        backward_kernel,
        out_shape=(
            jax.ShapeDtypeStruct((2 * n, HEAD_DIM), F32),
            jax.ShapeDtypeStruct((2 * n, HEAD_DIM), F32),
            jax.ShapeDtypeStruct(kv.shape, BF16),
        ),
        in_specs=[vmem] * 8,
        out_specs=(vmem,) * 3,
        scratch_shapes=[
            pltpu.VMEM((8, 2 * n), F32),
            pltpu.VMEM((8, 2 * n), F32),
            pltpu.VMEM((HEAD_DIM, 2 * n), F32),
        ],
        cost_estimate=pl.CostEstimate(
            flops=20 * n * KEYS * HEAD_DIM, transcendentals=2 * n * KEYS, bytes_accessed=5 << 20
        ),
        compiler_params=pltpu.CompilerParams(vmem_limit_bytes=VMEM_LIMIT),
    )(q, q2, g, g2, kv, stat, stat2, half)


def join_kernel(keep_ref, recv_ref, terms_ref, out_ref, dq_ref, dk_ref, dv_ref):
    n = out_ref.shape[0]
    out_ref[...] = (keep_ref[:n, :] + recv_ref[:n, :]).astype(BF16)
    dq_ref[...] = (keep_ref[n:, :] + recv_ref[n:, :]).astype(BF16)
    total = jnp.sum(terms_ref[...].astype(F32), axis=0).astype(BF16)
    dk_ref[...] = total[:ROWS, :]
    dv_ref[...] = total[ROWS:, :]


def join(keep, recv, total):
    n = keep.shape[0] // 2
    vmem = pl.BlockSpec(memory_space=pltpu.VMEM)
    return pl.pallas_call(
        join_kernel,
        out_shape=tuple(jax.ShapeDtypeStruct((m, HEAD_DIM), BF16) for m in (n, n, ROWS, ROWS)),
        in_specs=[vmem] * 3,
        out_specs=(vmem,) * 4,
        compiler_params=pltpu.CompilerParams(vmem_limit_bytes=8 << 20),
    )(keep, recv, total)


def swap_cores(a):
    return lax.ppermute(a, "c", [(0, 1), (1, 0)])


def exchange(a):
    return lax.all_to_all(a, CHIPS, 0, 0, tiled=True)


def step(queries, keys, values, out_grad):
    q = queries.reshape(-1, HEAD_DIM)
    g = out_grad.reshape(-1, HEAD_DIM)
    q2, g2 = swap_cores(q), swap_cores(g)
    kv = jnp.concatenate([keys[:, 0, :], values[:, 0, :]], axis=0)
    kv, q2, g2 = lax.optimization_barrier((jnp.broadcast_to(kv[None], (NCHIP,) + kv.shape), q2, g2))
    kv = exchange(kv)
    stat, half = forward(q, q2, g, g2, kv)
    keep, send, dkv = backward(q, q2, g, g2, kv, stat, swap_cores(stat), half)
    recv = swap_cores(send)
    terms = exchange(dkv)
    out, dq, dk, dv = join(keep, recv, terms)
    return (
        out.reshape(queries.shape),
        dq.reshape(queries.shape),
        dk.reshape(keys.shape),
        dv.reshape(values.shape),
    )


def solution(mesh):
    fine = Mesh(mesh.devices.reshape(4, 2, 2, 2, 8), CHIPS + ("c", "z"))
    spec = P(CHIPS + ("c",), "z", None)
    return jax.shard_map(
        step,
        mesh=fine,
        in_specs=(spec,) * 4,
        out_specs=(spec,) * 4,
        check_vma=False,
    )
```

```python
import math

import jax
import jax.numpy as jnp
from jax import lax
from jax.experimental import pallas as pl
from jax.experimental.pallas import tpu as pltpu
from jax.sharding import Mesh, PartitionSpec as P


HEAD_DIM = 128
SCALE = HEAD_DIM ** (-0.5)
EXP2_SCALE = SCALE * math.log2(math.e)
LOG2E = math.log2(math.e)
CHIPS = ("x", "yl", "yh")
NCHIP = 16
ROWS = 128
KEYS = NCHIP * ROWS
QB = 256
KF = 512
KB = 512
VMEM_LIMIT = 32 << 20
F32 = jnp.float32
BF16 = jnp.bfloat16


def dot(a, b):
    return jnp.dot(a, b, preferred_element_type=F32)


def dot_t(a, b):
    return lax.dot_general(a, b, (((1,), (1,)), ((), ())), preferred_element_type=F32)


def span(b):
    return slice(b * QB, (b + 1) * QB)


def forward_kernel(q_ref, q2_ref, g_ref, g2_ref, kv_ref, mark_ref, stat_ref, half_ref, s0, s1):
    own_rows = q_ref.shape[0]
    rows = 2 * own_rows

    def body(q_all, k_all, vt):
        q_all[:own_rows, :] = q_ref[...]
        q_all[own_rows:, :] = q2_ref[...]
        vt[HEAD_DIM:, :] = jnp.ones((vt.shape[0] - HEAD_DIM, KEYS), BF16)
        for b in range(NCHIP):
            block = slice(b * ROWS, (b + 1) * ROWS)
            k_all[block, :] = kv_ref[b, :ROWS, :]
            vt[:HEAD_DIM, block] = jnp.transpose(kv_ref[b, ROWS:, :])
        stat_ref[...] = jnp.zeros_like(stat_ref)

        def finish(b, acc, peak):
            qs = span(b)
            total = acc[HEAD_DIM:HEAD_DIM + 1, :]
            out_t = acc[:HEAD_DIM, :] * (1.0 / total)
            half, lo = divmod(b * QB, own_rows)
            local = slice(lo, lo + QB)
            grad_t = jnp.transpose((g_ref, g2_ref)[half][local, :].astype(F32))
            stat_ref[0:1, qs] = peak
            stat_ref[1:2, qs] = total
            stat_ref[2:3, qs] = jnp.sum(grad_t * out_t, axis=0, keepdims=True)
            half_ref[:, qs] = out_t

        s_bufs = (s0, s1)
        peak = None
        for stage in range(rows // QB + 1):
            old_peak = peak
            top = None
            acc = None
            for lo in range(0, KEYS, KF):
                if stage < rows // QB:
                    s = dot_t(k_all[lo:lo + KF, :], q_all[span(stage), :])
                    s_bufs[stage % 2][lo:lo + KF, :] = s
                    part = jnp.max(s.reshape(KF // 8, 8, QB), axis=0)
                    top = part if top is None else jnp.maximum(top, part)
                if stage > 0:
                    b = stage - 1
                    p = jnp.exp2(s_bufs[b % 2][lo:lo + KF, :] * EXP2_SCALE - old_peak).astype(BF16)
                    term = dot(vt[:, lo:lo + KF], p)
                    acc = term if acc is None else acc + term
            if stage < rows // QB:
                peak = jnp.max(top, axis=0, keepdims=True) * EXP2_SCALE
            if stage > 0:
                finish(stage - 1, acc, old_peak)

    pl.run_scoped(
        body,
        pltpu.VMEM((rows, HEAD_DIM), BF16),
        pltpu.VMEM((KEYS, HEAD_DIM), BF16),
        pltpu.VMEM((HEAD_DIM + 16, KEYS), BF16),
    )


def backward_kernel(
    q_ref, q2_ref, g_ref, g2_ref, kv_ref, stat_ref, stat2_ref, half_ref,
    keep_ref, send_ref, dkv_ref,
    lse, dots, dqt,
):
    own_rows = q_ref.shape[0]
    rows = 2 * own_rows
    nq = rows // QB
    per = KB // ROWS
    chunks = KEYS // KB

    def body(q_all, g_all, k_all, v_all, kt, p0, p1, ds0, ds1):
        q_all[:own_rows, :] = q_ref[...]
        q_all[own_rows:, :] = q2_ref[...]
        g_all[:own_rows, :] = g_ref[...]
        g_all[own_rows:, :] = g2_ref[...]
        for b in range(NCHIP):
            block = slice(b * ROWS, (b + 1) * ROWS)
            k = kv_ref[b, :ROWS, :]
            k_all[block, :] = k
            v_all[block, :] = kv_ref[b, ROWS:, :]
            kt[:, block] = jnp.transpose(k)

        for half in range(2):
            here = slice(half * own_rows, (half + 1) * own_rows)
            there = slice((1 - half) * own_rows, (2 - half) * own_rows)
            peak_a, peak_b = stat_ref[0:1, here], stat2_ref[0:1, there]
            peak = jnp.maximum(peak_a, peak_b)
            total_a = stat_ref[1:2, here] * jnp.exp2(peak_a - peak)
            total_b = stat2_ref[1:2, there] * jnp.exp2(peak_b - peak)
            total = total_a + total_b
            weight_a = total_a / total
            lse[:, here] = jnp.broadcast_to(peak + jnp.log(total) * LOG2E, (8, own_rows))
            dots[:, here] = jnp.broadcast_to(
                weight_a * stat_ref[2:3, here] + total_b / total * stat2_ref[2:3, there], (8, own_rows)
            )
            for lo in range(0, own_rows, QB):
                at = half * own_rows + lo
                (keep_ref, send_ref)[half][lo:lo + QB, :] = jnp.transpose(
                    half_ref[:, at:at + QB] * weight_a[:, lo:lo + QB]
                )

        dqt[...] = jnp.zeros_like(dqt)
        p_bufs, ds_bufs = (p0, p1), (ds0, ds1)

        def score_grad(c, b):
            keys, qs = slice(c * KB, (c + 1) * KB), span(b)
            s = dot_t(k_all[keys, :], q_all[qs, :])
            dp = dot_t(v_all[keys, :], g_all[qs, :])
            p = jnp.exp2(s * EXP2_SCALE - lse[0:1, qs])
            p_bufs[c % 2][:, qs] = p.astype(BF16)
            ds_bufs[c % 2][:, qs] = (p * (dp - dots[0:1, qs])).astype(BF16)

        def store(c, part, lo, value):
            first = c * per + lo // ROWS
            n = value.shape[0] // ROWS
            dkv_ref[first:first + n, part * ROWS:(part + 1) * ROWS, :] = value.astype(BF16).reshape(
                n, ROWS, HEAD_DIM
            )

        def value_grad(c, lo):
            store(c, 1, lo, dot(p_bufs[c % 2][lo:lo + KB // 2, :], g_all[...]))

        def key_grad(c, lo):
            store(c, 0, lo, dot(ds_bufs[c % 2][lo:lo + KB // 2, :], q_all[...]) * SCALE)

        def query_grad(c, b):
            dqt[:, span(b)] += dot(kt[:, c * KB:(c + 1) * KB], ds_bufs[c % 2][:, span(b)])

        for c in range(chunks + 1):
            prior = c - 1
            for b in range(nq):
                if c < chunks:
                    score_grad(c, b)
                if prior >= 0:
                    if b < 2:
                        value_grad(prior, b * (KB // 2))
                    elif b < 4:
                        key_grad(prior, (b - 2) * (KB // 2))
                    else:
                        query_grad(prior, 2 * b - 8)
                        query_grad(prior, 2 * b - 7)
        for b in range(nq):
            half, lo = divmod(b * QB, own_rows)
            at = own_rows + lo
            (keep_ref, send_ref)[half][at:at + QB, :] = jnp.transpose(dqt[:, span(b)]) * SCALE

    pl.run_scoped(
        body,
        pltpu.VMEM((rows, HEAD_DIM), BF16),
        pltpu.VMEM((rows, HEAD_DIM), BF16),
        pltpu.VMEM((KEYS, HEAD_DIM), BF16),
        pltpu.VMEM((KEYS, HEAD_DIM), BF16),
        pltpu.VMEM((HEAD_DIM, KEYS), BF16),
        *[pltpu.VMEM((KB, rows), BF16) for _ in range(4)],
    )


def forward(q, q2, g, g2, kv, mark):
    n = q.shape[0]
    vmem = pl.BlockSpec(memory_space=pltpu.VMEM)
    return pl.pallas_call(
        forward_kernel,
        out_shape=(
            jax.ShapeDtypeStruct((8, 2 * n), F32),
            jax.ShapeDtypeStruct((HEAD_DIM, 2 * n), F32),
        ),
        in_specs=[vmem] * 6,
        out_specs=(vmem,) * 2,
        scratch_shapes=[pltpu.VMEM((KEYS, QB), F32), pltpu.VMEM((KEYS, QB), F32)],
        cost_estimate=pl.CostEstimate(
            flops=8 * n * KEYS * HEAD_DIM, transcendentals=2 * n * KEYS, bytes_accessed=3 << 20
        ),
        compiler_params=pltpu.CompilerParams(vmem_limit_bytes=VMEM_LIMIT),
    )(q, q2, g, g2, kv, mark)


def backward(q, q2, g, g2, kv, stat, stat2, half):
    n = q.shape[0]
    vmem = pl.BlockSpec(memory_space=pltpu.VMEM)
    return pl.pallas_call(
        backward_kernel,
        out_shape=(
            jax.ShapeDtypeStruct((2 * n, HEAD_DIM), F32),
            jax.ShapeDtypeStruct((2 * n, HEAD_DIM), F32),
            jax.ShapeDtypeStruct(kv.shape, BF16),
        ),
        in_specs=[vmem] * 8,
        out_specs=(vmem,) * 3,
        scratch_shapes=[
            pltpu.VMEM((8, 2 * n), F32),
            pltpu.VMEM((8, 2 * n), F32),
            pltpu.VMEM((HEAD_DIM, 2 * n), F32),
        ],
        cost_estimate=pl.CostEstimate(
            flops=20 * n * KEYS * HEAD_DIM, transcendentals=2 * n * KEYS, bytes_accessed=5 << 20
        ),
        compiler_params=pltpu.CompilerParams(vmem_limit_bytes=VMEM_LIMIT),
    )(q, q2, g, g2, kv, stat, stat2, half)


def join_kernel(keep_ref, recv_ref, terms_ref, out_ref, dq_ref, dk_ref, dv_ref):
    n = out_ref.shape[0]
    out_ref[...] = (keep_ref[:n, :] + recv_ref[:n, :]).astype(BF16)
    dq_ref[...] = (keep_ref[n:, :] + recv_ref[n:, :]).astype(BF16)
    total = jnp.sum(terms_ref[...].astype(F32), axis=0).astype(BF16)
    dk_ref[...] = total[:ROWS, :]
    dv_ref[...] = total[ROWS:, :]


def join(keep, recv, total):
    n = keep.shape[0] // 2
    vmem = pl.BlockSpec(memory_space=pltpu.VMEM)
    return pl.pallas_call(
        join_kernel,
        out_shape=tuple(jax.ShapeDtypeStruct((m, HEAD_DIM), BF16) for m in (n, n, ROWS, ROWS)),
        in_specs=[vmem] * 3,
        out_specs=(vmem,) * 4,
        compiler_params=pltpu.CompilerParams(vmem_limit_bytes=8 << 20),
    )(keep, recv, total)


def swap_cores(a):
    return lax.ppermute(a, "c", [(0, 1), (1, 0)])


def exchange(a):
    return lax.all_to_all(a, CHIPS, 0, 0, tiled=True)


def step(queries, keys, values, out_grad):
    q = queries.reshape(-1, HEAD_DIM)
    g = out_grad.reshape(-1, HEAD_DIM)
    q2 = swap_cores(q)
    g2 = swap_cores(g)
    kv = jnp.concatenate([keys[:, 0, :], values[:, 0, :]], axis=0)
    kv = exchange(jnp.broadcast_to(kv[None], (NCHIP,) + kv.shape))
    mark = jnp.max(kv[:1, :16, :], axis=0)
    stat, half = forward(q, q2, g, g2, kv, mark)
    keep, send, dkv = backward(q, q2, g, g2, kv, stat, swap_cores(stat), half)
    recv = swap_cores(send)
    terms = exchange(dkv)
    out, dq, dk, dv = join(keep, recv, terms)
    return (
        out.reshape(queries.shape),
        dq.reshape(queries.shape),
        dk.reshape(keys.shape),
        dv.reshape(values.shape),
    )


def solution(mesh):
    fine = Mesh(mesh.devices.reshape(4, 2, 2, 2, 8), CHIPS + ("c", "z"))
    spec = P(CHIPS + ("c",), "z", None)
    return jax.shard_map(
        step,
        mesh=fine,
        in_specs=(spec,) * 4,
        out_specs=(spec,) * 4,
        check_vma=False,
    )
```

```python
import math

import jax
import jax.numpy as jnp
from jax import lax
from jax.experimental import pallas as pl
from jax.experimental.pallas import tpu as pltpu
from jax.sharding import Mesh, PartitionSpec as P


HEAD_DIM = 128
SCALE = HEAD_DIM ** (-0.5)
EXP2_SCALE = SCALE * math.log2(math.e)
LOG2E = math.log2(math.e)
CHIPS = ("x", "yl", "yh")
NCHIP = 16
ROWS = 128
KEYS = NCHIP * ROWS
QB = 256
KF = 512
KB = 1024
VMEM_LIMIT = 32 << 20
F32 = jnp.float32
BF16 = jnp.bfloat16


def dot(a, b):
    return jnp.dot(a, b, preferred_element_type=F32)


def dot_t(a, b):
    return lax.dot_general(a, b, (((1,), (1,)), ((), ())), preferred_element_type=F32)


def span(b):
    return slice(b * QB, (b + 1) * QB)


def forward_kernel(q_ref, q2_ref, g_ref, g2_ref, kv_ref, mark_ref, stat_ref, half_ref, s0, s1):
    own_rows = q_ref.shape[0]
    rows = 2 * own_rows

    def body(q_all, k_all, vt):
        q_all[:own_rows, :] = q_ref[...]
        q_all[own_rows:, :] = q2_ref[...]
        vt[HEAD_DIM:, :] = jnp.ones((vt.shape[0] - HEAD_DIM, KEYS), BF16)
        for b in range(NCHIP):
            block = slice(b * ROWS, (b + 1) * ROWS)
            k_all[block, :] = kv_ref[b, :ROWS, :]
            vt[:HEAD_DIM, block] = jnp.transpose(kv_ref[b, ROWS:, :])
        stat_ref[...] = jnp.zeros_like(stat_ref)

        def finish(b, acc, peak):
            qs = span(b)
            total = acc[HEAD_DIM:HEAD_DIM + 1, :]
            out_t = acc[:HEAD_DIM, :] * (1.0 / total)
            half, lo = divmod(b * QB, own_rows)
            local = slice(lo, lo + QB)
            grad_t = jnp.transpose((g_ref, g2_ref)[half][local, :].astype(F32))
            stat_ref[0:1, qs] = peak
            stat_ref[1:2, qs] = total
            stat_ref[2:3, qs] = jnp.sum(grad_t * out_t, axis=0, keepdims=True)
            half_ref[:, qs] = out_t

        s_bufs = (s0, s1)
        peak = None
        for stage in range(rows // QB + 1):
            old_peak = peak
            top = None
            acc = None
            for lo in range(0, KEYS, KF):
                if stage < rows // QB:
                    s = dot_t(k_all[lo:lo + KF, :], q_all[span(stage), :])
                    s_bufs[stage % 2][lo:lo + KF, :] = s
                    part = jnp.max(s.reshape(KF // 8, 8, QB), axis=0)
                    top = part if top is None else jnp.maximum(top, part)
                if stage > 0:
                    b = stage - 1
                    p = jnp.exp2(s_bufs[b % 2][lo:lo + KF, :] * EXP2_SCALE - old_peak).astype(BF16)
                    term = dot(vt[:, lo:lo + KF], p)
                    acc = term if acc is None else acc + term
            if stage < rows // QB:
                peak = jnp.max(top, axis=0, keepdims=True) * EXP2_SCALE
            if stage > 0:
                finish(stage - 1, acc, old_peak)

    pl.run_scoped(
        body,
        pltpu.VMEM((rows, HEAD_DIM), BF16),
        pltpu.VMEM((KEYS, HEAD_DIM), BF16),
        pltpu.VMEM((HEAD_DIM + 16, KEYS), BF16),
    )


def backward_kernel(
    q_ref, q2_ref, g_ref, g2_ref, kv_ref, stat_ref, stat2_ref, half_ref,
    keep_ref, send_ref, dkv_ref,
    lse, dots, dqt,
):
    own_rows = q_ref.shape[0]
    rows = 2 * own_rows
    nq = rows // QB
    per = KB // ROWS
    chunks = KEYS // KB

    def body(q_all, g_all, k_all, v_all, kt, p0, p1, ds0, ds1):
        q_all[:own_rows, :] = q_ref[...]
        q_all[own_rows:, :] = q2_ref[...]
        g_all[:own_rows, :] = g_ref[...]
        g_all[own_rows:, :] = g2_ref[...]
        for b in range(NCHIP):
            block = slice(b * ROWS, (b + 1) * ROWS)
            k = kv_ref[b, :ROWS, :]
            k_all[block, :] = k
            v_all[block, :] = kv_ref[b, ROWS:, :]
            kt[:, block] = jnp.transpose(k)

        for half in range(2):
            here = slice(half * own_rows, (half + 1) * own_rows)
            there = slice((1 - half) * own_rows, (2 - half) * own_rows)
            peak_a, peak_b = stat_ref[0:1, here], stat2_ref[0:1, there]
            peak = jnp.maximum(peak_a, peak_b)
            total_a = stat_ref[1:2, here] * jnp.exp2(peak_a - peak)
            total_b = stat2_ref[1:2, there] * jnp.exp2(peak_b - peak)
            total = total_a + total_b
            weight_a = total_a / total
            lse[:, here] = jnp.broadcast_to(peak + jnp.log(total) * LOG2E, (8, own_rows))
            dots[:, here] = jnp.broadcast_to(
                weight_a * stat_ref[2:3, here] + total_b / total * stat2_ref[2:3, there], (8, own_rows)
            )
            for lo in range(0, own_rows, QB):
                at = half * own_rows + lo
                (keep_ref, send_ref)[half][lo:lo + QB, :] = jnp.transpose(
                    half_ref[:, at:at + QB] * weight_a[:, lo:lo + QB]
                )

        dqt[...] = jnp.zeros_like(dqt)
        p_bufs, ds_bufs = (p0, p1), (ds0, ds1)

        def score_grad(c, b):
            keys, qs = slice(c * KB, (c + 1) * KB), span(b)
            s = dot_t(k_all[keys, :], q_all[qs, :])
            dp = dot_t(v_all[keys, :], g_all[qs, :])
            p = jnp.exp2(s * EXP2_SCALE - lse[0:1, qs])
            p_bufs[c % 2][:, qs] = p.astype(BF16)
            ds_bufs[c % 2][:, qs] = (p * (dp - dots[0:1, qs])).astype(BF16)

        def store(c, part, lo, value):
            first = c * per + lo // ROWS
            n = value.shape[0] // ROWS
            dkv_ref[first:first + n, part * ROWS:(part + 1) * ROWS, :] = value.astype(BF16).reshape(
                n, ROWS, HEAD_DIM
            )

        def value_grad(c, lo):
            store(c, 1, lo, dot(p_bufs[c % 2][lo:lo + KB, :], g_all[...]))

        def key_grad(c, lo):
            store(c, 0, lo, dot(ds_bufs[c % 2][lo:lo + KB, :], q_all[...]) * SCALE)

        def query_grad(c, b):
            dqt[:, span(b)] += dot(kt[:, c * KB:(c + 1) * KB], ds_bufs[c % 2][:, span(b)])

        for c in range(chunks + 1):
            prior = c - 1
            for b in range(nq):
                if c < chunks:
                    score_grad(c, b)
                if prior >= 0:
                    if b == 0:
                        value_grad(prior, 0)
                        key_grad(prior, 0)
                    elif b >= 4:
                        query_grad(prior, 2 * b - 8)
                        query_grad(prior, 2 * b - 7)
        for b in range(nq):
            half, lo = divmod(b * QB, own_rows)
            at = own_rows + lo
            (keep_ref, send_ref)[half][at:at + QB, :] = jnp.transpose(dqt[:, span(b)]) * SCALE

    pl.run_scoped(
        body,
        pltpu.VMEM((rows, HEAD_DIM), BF16),
        pltpu.VMEM((rows, HEAD_DIM), BF16),
        pltpu.VMEM((KEYS, HEAD_DIM), BF16),
        pltpu.VMEM((KEYS, HEAD_DIM), BF16),
        pltpu.VMEM((HEAD_DIM, KEYS), BF16),
        *[pltpu.VMEM((KB, rows), BF16) for _ in range(4)],
    )


def forward(q, q2, g, g2, kv, mark):
    n = q.shape[0]
    vmem = pl.BlockSpec(memory_space=pltpu.VMEM)
    return pl.pallas_call(
        forward_kernel,
        out_shape=(
            jax.ShapeDtypeStruct((8, 2 * n), F32),
            jax.ShapeDtypeStruct((HEAD_DIM, 2 * n), F32),
        ),
        in_specs=[vmem] * 6,
        out_specs=(vmem,) * 2,
        scratch_shapes=[pltpu.VMEM((KEYS, QB), F32), pltpu.VMEM((KEYS, QB), F32)],
        cost_estimate=pl.CostEstimate(
            flops=8 * n * KEYS * HEAD_DIM, transcendentals=2 * n * KEYS, bytes_accessed=3 << 20
        ),
        compiler_params=pltpu.CompilerParams(vmem_limit_bytes=VMEM_LIMIT),
    )(q, q2, g, g2, kv, mark)


def backward(q, q2, g, g2, kv, stat, stat2, half):
    n = q.shape[0]
    vmem = pl.BlockSpec(memory_space=pltpu.VMEM)
    return pl.pallas_call(
        backward_kernel,
        out_shape=(
            jax.ShapeDtypeStruct((2 * n, HEAD_DIM), F32),
            jax.ShapeDtypeStruct((2 * n, HEAD_DIM), F32),
            jax.ShapeDtypeStruct(kv.shape, BF16),
        ),
        in_specs=[vmem] * 8,
        out_specs=(vmem,) * 3,
        scratch_shapes=[
            pltpu.VMEM((8, 2 * n), F32),
            pltpu.VMEM((8, 2 * n), F32),
            pltpu.VMEM((HEAD_DIM, 2 * n), F32),
        ],
        cost_estimate=pl.CostEstimate(
            flops=20 * n * KEYS * HEAD_DIM, transcendentals=2 * n * KEYS, bytes_accessed=5 << 20
        ),
        compiler_params=pltpu.CompilerParams(vmem_limit_bytes=VMEM_LIMIT),
    )(q, q2, g, g2, kv, stat, stat2, half)


def join_kernel(keep_ref, recv_ref, terms_ref, out_ref, dq_ref, dk_ref, dv_ref):
    n = out_ref.shape[0]
    out_ref[...] = (keep_ref[:n, :] + recv_ref[:n, :]).astype(BF16)
    dq_ref[...] = (keep_ref[n:, :] + recv_ref[n:, :]).astype(BF16)
    total = jnp.sum(terms_ref[...].astype(F32), axis=0).astype(BF16)
    dk_ref[...] = total[:ROWS, :]
    dv_ref[...] = total[ROWS:, :]


def join(keep, recv, total):
    n = keep.shape[0] // 2
    vmem = pl.BlockSpec(memory_space=pltpu.VMEM)
    return pl.pallas_call(
        join_kernel,
        out_shape=tuple(jax.ShapeDtypeStruct((m, HEAD_DIM), BF16) for m in (n, n, ROWS, ROWS)),
        in_specs=[vmem] * 3,
        out_specs=(vmem,) * 4,
        compiler_params=pltpu.CompilerParams(vmem_limit_bytes=8 << 20),
    )(keep, recv, total)


def swap_cores(a):
    return lax.ppermute(a, "c", [(0, 1), (1, 0)])


def exchange(a):
    return lax.all_to_all(a, CHIPS, 0, 0, tiled=True)


def step(queries, keys, values, out_grad):
    q = queries.reshape(-1, HEAD_DIM)
    g = out_grad.reshape(-1, HEAD_DIM)
    q2 = swap_cores(q)
    g2 = swap_cores(g)
    kv = jnp.concatenate([keys[:, 0, :], values[:, 0, :]], axis=0)
    kv = exchange(jnp.broadcast_to(kv[None], (NCHIP,) + kv.shape))
    mark = jnp.max(kv[:1, :16, :], axis=0)
    stat, half = forward(q, q2, g, g2, kv, mark)
    keep, send, dkv = backward(q, q2, g, g2, kv, stat, swap_cores(stat), half)
    recv = swap_cores(send)
    terms = exchange(dkv)
    out, dq, dk, dv = join(keep, recv, terms)
    return (
        out.reshape(queries.shape),
        dq.reshape(queries.shape),
        dk.reshape(keys.shape),
        dv.reshape(values.shape),
    )


def solution(mesh):
    fine = Mesh(mesh.devices.reshape(4, 2, 2, 2, 8), CHIPS + ("c", "z"))
    spec = P(CHIPS + ("c",), "z", None)
    return jax.shard_map(
        step,
        mesh=fine,
        in_specs=(spec,) * 4,
        out_specs=(spec,) * 4,
        check_vma=False,
    )
```
